32 devices in a mesh: dp: 4 (over y, x), px: 4 (over z), py: 2 (over core).
Axes of the slice: x: 2, y: 2, z: 4, core: 2. Of those that a mesh axis runs over, the one named last changes fastest.
Arguments:
- fields: bfloat16 [4, 16, 16, 32, 256], P('dp', 'px', 'py'), may hold values from -6 to 6
- cotangent: bfloat16 [4, 16, 16, 32, 256], P('dp', 'px', 'py'), may hold values from -6 to 6
- first_weight: bfloat16 [6912, 256], replicated, may hold values from -0.078125 to 0.078125
- second_weight: bfloat16 [6912, 256], replicated, may hold values from -0.078125 to 0.078125
Outputs:
- output: bfloat16 [4, 16, 16, 32, 256], P('dp', 'px', 'py')
- field_grad: bfloat16 [4, 16, 16, 32, 256], P('dp', 'px', 'py')
- first_grad: float32 [6912, 256], P('dp', ('px', 'py'))
- second_grad: float32 [6912, 256], P('dp', ('px', 'py'))
The draws below stay inside these ranges and needn't reach their ends.
All inputs are finite; a program needn't handle non-finite values.
Results may differ from the reference program's by a relative error of at most 0.0033.
Values may be sent and summed in bfloat16 or wider, within the bound.
A program may use at most 128 MiB of HBM per device.

```python
import jax
import jax.numpy as jnp
from jax import lax

C = 256
KC = 6912
ROLL = 4
NX = 16
NY = 16
NZ = 32


def shard_levels(stream_key, shape, shards, low, top_value):
    factor_of, own = 1.0, jax.random.fold_in(stream_key, 6)
    for dim, blocks in shards:
        draws = jnp.exp(jax.random.uniform(jax.random.fold_in(own, dim), (blocks,), jnp.float32, low / len(shards), top_value / len(shards)))
        factor_of = factor_of * jnp.repeat(draws, shape[dim] // blocks).reshape([-1 if axis == dim else 1 for axis in range(len(shape))])
    return factor_of


def centred(rng, dims, scale, most, split=(), dtype=jnp.bfloat16):
    loudness = shard_levels(rng, dims, split, -0.22, 0.18) if split else 1.0
    drawn = jax.random.normal(rng, dims, jnp.float32) * scale * loudness
    return jnp.minimum(jnp.maximum(drawn, -most), most).astype(dtype)


def setup_inputs(seed: int = 0) -> dict:
    key_of = jax.random.split(jax.random.key(seed), 5)
    return {
        "fields": centred(key_of[0], (ROLL, NX, NY, NZ, C), 1.0, 6.0, ((0, 4), (1, 4), (2, 2))),
        "cotangent": centred(key_of[1], (ROLL, NX, NY, NZ, C), 1.0, 6.0, ((0, 4), (1, 4), (2, 2))),
        "first_weight": centred(key_of[2], (KC, C), KC ** -0.5, 0.078125),
        "second_weight": centred(key_of[3], (KC, C), KC ** -0.5, 0.078125),
    }


def gelu_tanh(v):
    return jax.nn.gelu(v, approximate=True)

def padded_grid(field):
    return jnp.pad(field, ((1, 1), (1, 1), (1, 1), (0, 0)))

def window(padded, start_x, start_y, start_z):
    size_x, size_y, size_z, width = padded.shape
    block = padded[start_x:start_x + size_x - 2, start_y:start_y + size_y - 2, start_z:start_z + size_z - 2, :]
    return block.reshape(-1, width)

def conv_forward(padded, weight):
    width = padded.shape[-1]
    total = None
    for offset in range(27):
        first, second, third = (offset // 9, offset // 3 % 3, offset % 3)
        block = weight[offset * width:(offset + 1) * width]
        term = jnp.dot(window(padded, first, second, third), block, preferred_element_type=jnp.float32)
        total = term if total is None else total + term
    return total

def conv_transposed(padded, weight):
    width = padded.shape[-1]
    total = None
    for offset in range(27):
        first, second, third = (offset // 9, offset // 3 % 3, offset % 3)
        block = weight[offset * width:(offset + 1) * width]
        rows = window(padded, 2 - first, 2 - second, 2 - third)
        term = lax.dot_general(rows, block, (((1,), (1,)), ((), ())), preferred_element_type=jnp.float32)
        total = term if total is None else total + term
    return total

def weight_terms(padded, grads):
    blocks = []
    for offset in range(27):
        first, second, third = (offset // 9, offset // 3 % 3, offset % 3)
        rows = window(padded, first, second, third)
        blocks.append(lax.dot_general(rows, grads, (((0,), (0,)), ((), ())), preferred_element_type=jnp.float32))
    return jnp.concatenate(blocks, axis=0)

def reference(fields, cotangent, first_weight, second_weight):

    def one_rollout(carry, pair):
        first_acc, second_acc = carry
        field_one, cot_one = pair
        shape = field_one.shape
        width = shape[-1]
        fields_padded = padded_grid(field_one)
        pre = conv_forward(fields_padded, first_weight)
        hidden = gelu_tanh(pre).astype(jnp.bfloat16)
        hidden_padded = padded_grid(hidden.reshape(shape))
        second_out = conv_forward(hidden_padded, second_weight)
        output = (field_one.reshape(-1, width).astype(jnp.float32) + second_out).astype(jnp.bfloat16).reshape(shape)
        cot_flat = cot_one.reshape(-1, width)
        hidden_grad = conv_transposed(padded_grid(cot_one), second_weight)
        second_acc = second_acc + weight_terms(hidden_padded, cot_flat)
        gelu_back = jax.vjp(gelu_tanh, pre)[1]
        pre_grad = gelu_back(hidden_grad)[0].astype(jnp.bfloat16)
        field_term = conv_transposed(padded_grid(pre_grad.reshape(shape)), first_weight)
        field_grad = (cot_flat.astype(jnp.float32) + field_term).astype(jnp.bfloat16).reshape(shape)
        first_acc = first_acc + weight_terms(fields_padded, pre_grad)
        return ((first_acc, second_acc), (output, field_grad))
    zeros = jnp.zeros((KC, C), jnp.float32)
    sums, outs = lax.scan(one_rollout, (zeros, zeros), (fields, cotangent))
    output, field_grad = outs
    return (output, field_grad, sums[0] / ROLL, sums[1] / ROLL)
```

```python
import functools

import jax
import jax.numpy as jnp
from jax import lax
from jax.experimental import pallas as pl
from jax.experimental.pallas import tpu as pltpu
from jax.sharding import PartitionSpec as P

MESH = pl.DeviceIdType.MESH
F32, BF16 = jnp.float32, jnp.bfloat16
DIRS = [(dx, dy) for dx in (-1, 0, 1) for dy in (-1, 0, 1) if dx or dy]
GELU_C = 0.7978845608028654
GELU_A = 0.044715


def gelu_parts(v):
    return jnp.tanh(GELU_C * (v + GELU_A * (v * v * v)))


def kernel(
    sizes,
    fields, cot, w1_hbm, w2_hbm,
    out_ref, fgrad_ref, g1_ref, g2_ref,
    w1, w2, p_f, p_c, p_h, p_g, z_a, z_b, z_c, lhs_f, lhs_h, pre,
    own, send_a, recv_a, recv_b, tot, send_z, recv_z,
    sem_w, halo_send, halo_recv, a_send, a_recv, b_send, b_recv, z_send, z_recv,
):
    ndp, npx, npy, rollouts = sizes
    nx, ny, nz, ch = fields.shape
    cells = nx * ny * nz
    half = ch // npy
    rows = own.shape[1] // ndp
    rpad = tot.shape[0]
    wid = recv_z.shape[2]
    nj = half // wid
    d, x, y = lax.axis_index("dp"), lax.axis_index("px"), lax.axis_index("py")

    load_w = [
        pltpu.make_async_copy(w1_hbm, w1, sem_w.at[0]),
        pltpu.make_async_copy(w2_hbm, w2, sem_w.at[1]),
    ]
    for copy in load_w:
        copy.start()

    barrier = pltpu.get_barrier_semaphore()
    for i in range(1, ndp):
        pl.semaphore_signal(
            barrier, inc=1, device_id=(lax.rem(d + i, ndp), x, y), device_id_type=MESH
        )
    for i in range(1, npx * npy):
        other = lax.rem(x * npy + y + i, npx * npy)
        pl.semaphore_signal(
            barrier, inc=1, device_id=(d, other // npy, lax.rem(other, npy)), device_id_type=MESH
        )
    pl.semaphore_wait(barrier, ndp - 1 + npx * npy - 1)

    def exists(dx, dy):
        return (x + dx >= 0) & (x + dx < npx) & (y + dy >= 0) & (y + dy < npy)

    def span_src(step, size, base):
        if step == 0:
            return pl.ds(base, size)
        return pl.ds(base if step < 0 else base + size - 1, 1)

    def span_dst(step, size):
        if step == 0:
            return pl.ds(1, size)
        return pl.ds(size + 1 if step < 0 else 0, 1)

    def halo_copy(which, src, base, padded, index):
        dx, dy = DIRS[index]
        return pltpu.make_async_remote_copy(
            src_ref=src.at[span_src(dx, nx, base), span_src(dy, ny, base)],
            dst_ref=padded.at[span_dst(dx, nx), span_dst(dy, ny)],
            send_sem=halo_send.at[which, index],
            recv_sem=halo_recv.at[which, index],
            device_id=(d, x + dx, y + dy),
            device_id_type=MESH,
        )

    def halo_start(which, src, base, padded):
        for index, (dx, dy) in enumerate(DIRS):
            @pl.when(exists(dx, dy))
            def _():
                halo_copy(which, src, base, padded, index).start()

            @pl.when(jnp.logical_not(exists(-dx, -dy)))
            def _():
                sx, sy = span_dst(dx, nx), span_dst(dy, ny)
                padded[sx, sy] = jnp.zeros((sx.size, sy.size, nz, ch), BF16)

    def halo_wait(which, src, base, padded):
        for index, (dx, dy) in enumerate(DIRS):
            @pl.when(exists(dx, dy))
            def _():
                halo_copy(which, src, base, padded, index).wait_send()

            @pl.when(exists(-dx, -dy))
            def _():
                halo_copy(which, src, base, padded, index).wait_recv()

    def build(padded, shifted):
        @pl.loop(0, nx + 2)
        def _(i):
            plane = padded[i]
            flat = plane.reshape((ny + 2) * nz, ch).astype(F32)
            place = lax.broadcasted_iota(jnp.int32, flat.shape, 0) % nz
            low = jnp.where(place == 0, 0.0, pltpu.roll(flat, 1, 0))
            high = jnp.where(place == nz - 1, 0.0, pltpu.roll(flat, flat.shape[0] - 1, 0))
            shifted[i, :, :, 0:ch] = low.astype(BF16).reshape(plane.shape)
            shifted[i, :, :, ch : 2 * ch] = plane
            shifted[i, :, :, 2 * ch : 3 * ch] = high.astype(BF16).reshape(plane.shape)

    tile = ny * nz

    def conv(shifted, weight, flipped, finish):
        @pl.loop(0, nx)
        def _(i):
            total = None
            for a in range(3):
                for b in range(3):
                    first = (9 * a + 3 * b) * ch
                    if not flipped:
                        lhs = shifted[i + a, pl.ds(b, ny)].reshape(tile, 3 * ch)
                        term = jnp.dot(
                            lhs, weight[pl.ds(first, 3 * ch)], preferred_element_type=F32
                        )
                        total = term if total is None else total + term
                        continue
                    for c in range(3):
                        lhs = shifted[
                            i + 2 - a, pl.ds(2 - b, ny), :, pl.ds((2 - c) * ch, ch)
                        ].reshape(tile, ch)
                        term = lax.dot_general(
                            lhs,
                            weight[pl.ds(first + c * ch, ch)],
                            (((1,), (1,)), ((), ())),
                            preferred_element_type=F32,
                        )
                        total = term if total is None else total + term
            finish(i, total)

    partner = 1 - y

    def a_copy(which, step):
        part = pl.ds(pl.multiple_of(step * 3 * ch, 3 * ch), 3 * ch)
        return pltpu.make_async_remote_copy(
            src_ref=send_a.at[which, part],
            dst_ref=recv_a.at[which, part],
            send_sem=a_send.at[which, step],
            recv_sem=a_recv.at[which, step],
            device_id=(d, x, partner),
            device_id_type=MESH,
        )

    def weight_grad(which, lhs, shifted):
        @pl.loop(0, 9)
        def _(step):
            a, b = step // 3, step % 3
            rhs = shifted[pl.ds(2 - a, nx), pl.ds(2 - b, ny)].reshape(cells, 3 * ch)
            prod = jnp.dot(lhs[...], rhs, preferred_element_type=F32)
            for c in range(3):
                block = prod[:, (2 - c) * ch : (3 - c) * ch]
                here = pl.ds(pl.multiple_of(step * 3 * ch, ch) + c * ch, ch)
                low, high = block[:, :half], block[:, half:]
                own[which, here] = jnp.where(y == 0, low, high)
                send_a[which, here] = jnp.where(y == 0, high, low).astype(BF16)
            a_copy(which, step).start()

    def b_copy(which, hop):
        peer = lax.rem(d + hop, ndp)
        return pltpu.make_async_remote_copy(
            src_ref=send_a.at[which, pl.ds(pl.multiple_of(peer * rows, 16), rows)],
            dst_ref=recv_b.at[which, hop - 1],
            send_sem=b_send.at[which, hop - 1],
            recv_sem=b_recv.at[which, hop - 1],
            device_id=(peer, x, y),
            device_id_type=MESH,
        )

    def rows_start(which):
        @pl.loop(0, 9)
        def _(step):
            a_copy(which, step).wait()

        for hop in [*range(1, ndp), 0]:
            peer = lax.rem(d + hop, ndp)
            part = pl.ds(pl.multiple_of(peer * rows, 16), rows)
            total = own[which, part] + recv_a[which, part].astype(F32)
            if hop:
                send_a[which, part] = total.astype(BF16)
                b_copy(which, hop).start()
            else:
                own[which, part] = total

    def z_ids(j):
        owner = y * nj + j
        return owner // npy, lax.rem(owner, npy)

    def z_remote(which, j):
        px_o, py_o = z_ids(j)
        return pltpu.make_async_remote_copy(
            src_ref=send_z.at[which, pl.ds(j * wid, wid)],
            dst_ref=recv_z.at[which, x],
            send_sem=z_send.at[which, j],
            recv_sem=z_recv.at[which, x],
            device_id=(d, px_o, py_o),
            device_id_type=MESH,
        )

    def columns_start(which):
        for hop in range(1, ndp):
            b_copy(which, hop).wait()
        part = pl.ds(pl.multiple_of(d * rows, 16), rows)
        total = own[which, part]
        for hop in range(1, ndp):
            total = total + recv_b[which, hop - 1].astype(F32)
        tot[0:rows] = total
        if rpad > rows:
            tot[rows:rpad] = jnp.zeros((rpad - rows, half), F32)
        send_z[which] = tot[...].T.astype(BF16)
        for j in range(nj):
            px_o, py_o = z_ids(j)
            mine = (px_o == x) & (py_o == y)

            @pl.when(jnp.logical_not(mine))
            def _():
                z_remote(which, j).start()

            @pl.when(mine)
            def _():
                pltpu.make_async_copy(
                    send_z.at[which, pl.ds(j * wid, wid)], recv_z.at[which, x], z_recv.at[which, x]
                ).start()

    def finish_grad(which, grad):
        for j in range(nj):
            px_o, py_o = z_ids(j)

            @pl.when(jnp.logical_not((px_o == x) & (py_o == y)))
            def _():
                z_remote(which, j).wait_send()

        total = None
        for i in range(npx):
            pltpu.make_async_copy(
                recv_z.at[which, i], recv_z.at[which, i], z_recv.at[which, i]
            ).wait()
            term = recv_z[which, i].astype(F32)
            total = term if total is None else total + term
        grad[...] = total / rollouts

    halo_start(0, fields, 0, p_f)
    halo_start(1, cot, 0, p_c)
    p_f[pl.ds(1, nx), pl.ds(1, ny)] = fields[...]
    p_c[pl.ds(1, nx), pl.ds(1, ny)] = cot[...]
    lhs_f[...] = fields[...].reshape(cells, ch).T
    halo_wait(0, fields, 0, p_f)
    build(p_f, z_a)
    load_w[0].wait()

    def hidden_finish(i, total):
        pre[i] = total
        value = (total * (0.5 * (1.0 + gelu_parts(total)))).astype(BF16)
        p_h[i + 1, pl.ds(1, ny)] = value.reshape(ny, nz, ch)

    conv(z_a, w1, False, hidden_finish)
    halo_start(2, p_h, 1, p_h)
    lhs_h[...] = p_h[pl.ds(1, nx), pl.ds(1, ny)].reshape(cells, ch).T
    halo_wait(1, cot, 0, p_c)
    build(p_c, z_b)
    weight_grad(1, lhs_h, z_b)
    rows_start(1)
    load_w[1].wait()

    def grad_finish(i, total):
        v = pre[i]
        t = gelu_parts(v)
        slope = 0.5 * (1.0 + t) + (0.5 * v) * (1.0 - t * t) * (
            GELU_C * (1.0 + (3.0 * GELU_A) * (v * v))
        )
        p_g[i + 1, pl.ds(1, ny)] = (total * slope).astype(BF16).reshape(ny, nz, ch)

    conv(z_b, w2, True, grad_finish)
    halo_start(3, p_g, 1, p_g)
    halo_wait(2, p_h, 1, p_h)
    build(p_h, z_a)

    def out_finish(i, total):
        out_ref[i] = (
            (fields[i].reshape(tile, ch).astype(F32) + total).astype(BF16).reshape(ny, nz, ch)
        )

    conv(z_a, w2, False, out_finish)
    halo_wait(3, p_g, 1, p_g)
    build(p_g, z_c)
    weight_grad(0, lhs_f, z_c)
    rows_start(0)
    columns_start(1)

    def field_finish(i, total):
        fgrad_ref[i] = (
            (cot[i].reshape(tile, ch).astype(F32) + total).astype(BF16).reshape(ny, nz, ch)
        )

    conv(z_c, w1, True, field_finish)
    finish_grad(1, g2_ref)
    columns_start(0)
    finish_grad(0, g1_ref)


def body(sizes, fields, cotangent, first_weight, second_weight):
    ndp, npx, npy = sizes
    batch, nx, ny, nz, ch = fields.shape
    kc = first_weight.shape[0]
    half = ch // npy
    rows = kc // ndp
    rpad = -(-rows // 128) * 128
    wid = ch // (npx * npy)
    cells = nx * ny * nz
    vmem = pl.BlockSpec(memory_space=pltpu.VMEM)
    hbm = pl.BlockSpec(memory_space=pl.ANY)
    padded = pltpu.VMEM((nx + 2, ny + 2, nz, ch), BF16)
    shifted = pltpu.VMEM((nx + 2, ny + 2, nz, 3 * ch), BF16)
    dma = pltpu.SemaphoreType.DMA
    block = (nx, ny, nz, ch)
    out, fgrad, g1, g2 = pl.pallas_call(
        functools.partial(kernel, (ndp, npx, npy, batch * ndp)),
        out_shape=(
            jax.ShapeDtypeStruct(block, BF16),
            jax.ShapeDtypeStruct(block, BF16),
            jax.ShapeDtypeStruct((wid, rpad), F32),
            jax.ShapeDtypeStruct((wid, rpad), F32),
        ),
        in_specs=[vmem, vmem, hbm, hbm],
        out_specs=(vmem, vmem, vmem, vmem),
        scratch_shapes=[
            pltpu.VMEM((kc, ch), BF16),
            pltpu.VMEM((kc, ch), BF16),
            padded, padded, padded, padded,
            shifted, shifted, shifted,
            pltpu.VMEM((ch, cells), BF16),
            pltpu.VMEM((ch, cells), BF16),
            pltpu.VMEM((nx, ny * nz, ch), F32),
            pltpu.VMEM((2, kc, half), F32),
            pltpu.VMEM((2, kc, half), BF16),
            pltpu.VMEM((2, kc, half), BF16),
            pltpu.VMEM((2, ndp - 1, rows, half), BF16),
            pltpu.VMEM((rpad, half), F32),
            pltpu.VMEM((2, half, rpad), BF16),
            pltpu.VMEM((2, npx, wid, rpad), BF16),
            dma((2,)),
            dma((4, 8)), dma((4, 8)),
            dma((2, 9)), dma((2, 9)),
            dma((2, ndp - 1)), dma((2, ndp - 1)),
            dma((2, half // wid)), dma((2, npx)),
        ],
        compiler_params=pltpu.CompilerParams(
            collective_id=0, has_side_effects=True, vmem_limit_bytes=64000000
        ),
        name="closure",
    )(fields.reshape(block), cotangent.reshape(block), first_weight, second_weight)
    return (
        out.reshape(fields.shape),
        fgrad.reshape(fields.shape),
        g1[:, :rows].T,
        g2[:, :rows].T,
    )


def solution(mesh):
    sizes = tuple(mesh.shape[name] for name in ("dp", "px", "py"))
    placed = (P("dp", "px", "py", None, None), P("dp", "px", "py", None, None), P(), P())
    return jax.shard_map(
        functools.partial(body, sizes),
        mesh=mesh,
        in_specs=placed,
        out_specs=(
            P("dp", "px", "py", None, None),
            P("dp", "px", "py", None, None),
            P("dp", ("px", "py")),
            P("dp", ("px", "py")),
        ),
        check_vma=False,
    )
```

```python
import functools

import jax
import jax.numpy as jnp
from jax import lax
from jax.experimental import pallas as pl
from jax.experimental.pallas import tpu as pltpu
from jax.sharding import PartitionSpec as P

MESH = pl.DeviceIdType.MESH
F32, BF16 = jnp.float32, jnp.bfloat16
DIRS = [(dx, dy) for dx in (-1, 0, 1) for dy in (-1, 0, 1) if dx or dy]
GELU_C = 0.7978845608028654
GELU_A = 0.044715


def gelu_parts(v):
    return jnp.tanh(GELU_C * (v + GELU_A * (v * v * v)))


def dp_slots(ndp):
    db = 2 if ndp % 2 == 0 else 1
    da = ndp // db
    first = [(0, 0, hop, item) for hop in range(1, db) for item in [*range(1, da), 0]]
    other = [(0, 1, hop, item) for hop in range(1, da) for item in [*range(1, db), 0]]
    slots = [s for pair in zip(first, other) for s in pair]
    slots += first[len(other) :] + other[len(first) :]
    slots += [(1, 0, hop, 0) for hop in range(1, da)] + [(1, 1, hop, 0) for hop in range(1, db)]
    return (da, db), slots


def results(rows, out_in, fgrad_in, g1_in, g2_in, out_ref, fgrad_ref, g1_ref, g2_ref):
    out_ref[...] = out_in[...]
    fgrad_ref[...] = fgrad_in[...]
    g1_ref[...] = g1_in[:, :rows]
    g2_ref[...] = g2_in[:, :rows]


def kernel(
    sizes,
    fields, cot, w1_hbm, w2_hbm,
    out_ref, fgrad_ref, g1_ref, g2_ref,
    w1, w2, p_f, p_c, p_h, p_g, z_a, z_b, z_c, lhs_f, lhs_h, pre,
    own, send_a, recv_a, recv_b, tot, send_z, recv_z,
    sem_w, halo_send, halo_recv, a_send, a_recv, b_send, b_recv, z_send, z_recv,
):
    ndp, npx, npy, rollouts = sizes
    factors, b_slots = dp_slots(ndp)
    nx, ny, nz, ch = fields.shape
    cells = nx * ny * nz
    half = ch // npy
    rows = own.shape[1] // ndp
    rpad = tot.shape[0]
    wid = recv_z.shape[2]
    nj = half // wid
    d, x, y = lax.axis_index("dp"), lax.axis_index("px"), lax.axis_index("py")

    load_w = [
        pltpu.make_async_copy(w1_hbm, w1, sem_w.at[0]),
        pltpu.make_async_copy(w2_hbm, w2, sem_w.at[1]),
    ]
    for copy in load_w:
        copy.start()

    barrier = pltpu.get_barrier_semaphore()
    for i in range(1, ndp):
        pl.semaphore_signal(
            barrier, inc=1, device_id=(lax.rem(d + i, ndp), x, y), device_id_type=MESH
        )
    for i in range(1, npx * npy):
        other = lax.rem(x * npy + y + i, npx * npy)
        pl.semaphore_signal(
            barrier, inc=1, device_id=(d, other // npy, lax.rem(other, npy)), device_id_type=MESH
        )
    pl.semaphore_wait(barrier, ndp - 1 + npx * npy - 1)

    def exists(dx, dy):
        return (x + dx >= 0) & (x + dx < npx) & (y + dy >= 0) & (y + dy < npy)

    def span_src(step, size, base):
        if step == 0:
            return pl.ds(base, size)
        return pl.ds(base if step < 0 else base + size - 1, 1)

    def span_dst(step, size):
        if step == 0:
            return pl.ds(1, size)
        return pl.ds(size + 1 if step < 0 else 0, 1)

    def halo_copy(which, src, base, padded, index):
        dx, dy = DIRS[index]
        return pltpu.make_async_remote_copy(
            src_ref=src.at[span_src(dx, nx, base), span_src(dy, ny, base)],
            dst_ref=padded.at[span_dst(dx, nx), span_dst(dy, ny)],
            send_sem=halo_send.at[which, index],
            recv_sem=halo_recv.at[which, index],
            device_id=(d, x + dx, y + dy),
            device_id_type=MESH,
        )

    def halo_start(which, src, base, padded):
        for index, (dx, dy) in enumerate(DIRS):
            @pl.when(exists(dx, dy))
            def _():
                halo_copy(which, src, base, padded, index).start()

            @pl.when(jnp.logical_not(exists(-dx, -dy)))
            def _():
                sx, sy = span_dst(dx, nx), span_dst(dy, ny)
                padded[sx, sy] = jnp.zeros((sx.size, sy.size, nz, ch), BF16)

    def halo_wait(which, src, base, padded):
        for index, (dx, dy) in enumerate(DIRS):
            @pl.when(exists(dx, dy))
            def _():
                halo_copy(which, src, base, padded, index).wait_send()

            @pl.when(exists(-dx, -dy))
            def _():
                halo_copy(which, src, base, padded, index).wait_recv()

    def build(padded, shifted):
        @pl.loop(0, nx + 2)
        def _(i):
            plane = padded[i]
            flat = plane.reshape((ny + 2) * nz, ch).astype(F32)
            place = lax.broadcasted_iota(jnp.int32, flat.shape, 0) % nz
            low = jnp.where(place == 0, 0.0, pltpu.roll(flat, 1, 0))
            high = jnp.where(place == nz - 1, 0.0, pltpu.roll(flat, flat.shape[0] - 1, 0))
            shifted[i, :, :, 0:ch] = low.astype(BF16).reshape(plane.shape)
            shifted[i, :, :, ch : 2 * ch] = plane
            shifted[i, :, :, 2 * ch : 3 * ch] = high.astype(BF16).reshape(plane.shape)

    tile = ny * nz

    def conv(shifted, weight, flipped, finish, low=0, high=nx):
        @pl.loop(low, high)
        def _(i):
            total = None
            for a in range(3):
                for b in range(3):
                    first = (9 * a + 3 * b) * ch
                    if not flipped:
                        lhs = shifted[i + a, pl.ds(b, ny)].reshape(tile, 3 * ch)
                        term = jnp.dot(
                            lhs, weight[pl.ds(first, 3 * ch)], preferred_element_type=F32
                        )
                        total = term if total is None else total + term
                        continue
                    for c in range(3):
                        lhs = shifted[
                            i + 2 - a, pl.ds(2 - b, ny), :, pl.ds((2 - c) * ch, ch)
                        ].reshape(tile, ch)
                        term = lax.dot_general(
                            lhs,
                            weight[pl.ds(first + c * ch, ch)],
                            (((1,), (1,)), ((), ())),
                            preferred_element_type=F32,
                        )
                        total = term if total is None else total + term
            finish(i, total)

    partner = 1 - y

    def a_copy(which, step):
        part = pl.ds(pl.multiple_of(step * 3 * ch, 3 * ch), 3 * ch)
        return pltpu.make_async_remote_copy(
            src_ref=send_a.at[which, part],
            dst_ref=recv_a.at[which, part],
            send_sem=a_send.at[which, step],
            recv_sem=a_recv.at[which, step],
            device_id=(d, x, partner),
            device_id_type=MESH,
        )

    def weight_grad(which, lhs, shifted):
        @pl.loop(0, 9)
        def _(step):
            a, b = step // 3, step % 3
            rhs = shifted[pl.ds(2 - a, nx), pl.ds(2 - b, ny)].reshape(cells, 3 * ch)
            prod = jnp.dot(lhs[...], rhs, preferred_element_type=F32)
            for c in range(3):
                block = prod[:, (2 - c) * ch : (3 - c) * ch]
                here = pl.ds(pl.multiple_of(step * 3 * ch, ch) + c * ch, ch)
                low, high = block[:, :half], block[:, half:]
                own[which, here] = jnp.where(y == 0, low, high)
                send_a[which, here] = jnp.where(y == 0, high, low).astype(BF16)
            a_copy(which, step).start()

    da, db = factors
    part_rows = rows // 2
    ia, ib = d // db, lax.rem(d, db)

    def piece(a, b, side):
        first = (a * db + b) * rows + side * part_rows
        return pl.ds(pl.multiple_of(first, 16), part_rows)

    def ring(index, hop, count):
        return lax.rem(index + hop, count)

    def b_copy(which, phase, side, hop, item):
        along_b = (side == 0) == (phase == 0)
        if along_b:
            a, b = (ring(ia, item, da) if phase == 0 else ia), ring(ib, hop, db)
            peer = ia * db + b
        else:
            a, b = ring(ia, hop, da), (ring(ib, item, db) if phase == 0 else ib)
            peer = a * db + ib
        slot = b_slots.index((phase, side, hop, item))
        return piece(a, b, side), pltpu.make_async_remote_copy(
            src_ref=send_a.at[which, piece(a, b, side)],
            dst_ref=recv_b.at[which, slot],
            send_sem=b_send.at[which, slot],
            recv_sem=b_recv.at[which, slot],
            device_id=(peer, x, y),
            device_id_type=MESH,
        )

    def rows_start(which):
        @pl.loop(0, 9)
        def _(step):
            a_copy(which, step).wait()

        for slot in [s for s in b_slots if s[0] == 0]:
            part, copy = b_copy(which, *slot)
            send_a[which, part] = (own[which, part] + recv_a[which, part].astype(F32)).astype(BF16)
            copy.start()
        for side, count in ((0, da), (1, db)):
            for item in range(count):
                a, b = (ring(ia, item, da), ib) if side == 0 else (ia, ring(ib, item, db))
                part = piece(a, b, side)
                own[which, part] = own[which, part] + recv_a[which, part].astype(F32)

    def rows_next(which):
        for side, count, hops in ((0, da, db), (1, db, da)):
            for item in [*range(1, count), 0]:
                a, b = (ring(ia, item, da), ib) if side == 0 else (ia, ring(ib, item, db))
                part = piece(a, b, side)
                total = own[which, part]
                for hop in range(1, hops):
                    slot = (0, side, hop, item)
                    b_copy(which, *slot)[1].wait()
                    total = total + recv_b[which, b_slots.index(slot)].astype(F32)
                if item:
                    send_a[which, part] = total.astype(BF16)
                    b_copy(which, 1, side, item, 0)[1].start()
                else:
                    own[which, part] = total

    def z_ids(j):
        owner = y * nj + j
        return owner // npy, lax.rem(owner, npy)

    def z_remote(which, j):
        px_o, py_o = z_ids(j)
        return pltpu.make_async_remote_copy(
            src_ref=send_z.at[which, pl.ds(j * wid, wid)],
            dst_ref=recv_z.at[which, x],
            send_sem=z_send.at[which, j],
            recv_sem=z_recv.at[which, x],
            device_id=(d, px_o, py_o),
            device_id_type=MESH,
        )

    def columns_start(which):
        for side, hops in ((0, da), (1, db)):
            total = own[which, piece(ia, ib, side)]
            for hop in range(1, hops):
                slot = (1, side, hop, 0)
                b_copy(which, *slot)[1].wait()
                total = total + recv_b[which, b_slots.index(slot)].astype(F32)
            tot[side * part_rows : (side + 1) * part_rows] = total
        if rpad > rows:
            tot[rows:rpad] = jnp.zeros((rpad - rows, half), F32)
        send_z[which] = tot[...].T.astype(BF16)
        for j in range(nj):
            px_o, py_o = z_ids(j)
            mine = (px_o == x) & (py_o == y)

            @pl.when(jnp.logical_not(mine))
            def _():
                z_remote(which, j).start()

            @pl.when(mine)
            def _():
                pltpu.make_async_copy(
                    send_z.at[which, pl.ds(j * wid, wid)], recv_z.at[which, x], z_recv.at[which, x]
                ).start()

    def finish_grad(which, grad):
        for j in range(nj):
            px_o, py_o = z_ids(j)

            @pl.when(jnp.logical_not((px_o == x) & (py_o == y)))
            def _():
                z_remote(which, j).wait_send()

        total = None
        for i in range(npx):
            pltpu.make_async_copy(
                recv_z.at[which, i], recv_z.at[which, i], z_recv.at[which, i]
            ).wait()
            term = recv_z[which, i].astype(F32)
            total = term if total is None else total + term
        grad[...] = total / rollouts

    halo_start(0, fields, 0, p_f)
    halo_start(1, cot, 0, p_c)
    p_f[pl.ds(1, nx), pl.ds(1, ny)] = fields[...]
    p_c[pl.ds(1, nx), pl.ds(1, ny)] = cot[...]
    lhs_f[...] = fields[...].reshape(cells, ch).T
    halo_wait(0, fields, 0, p_f)
    build(p_f, z_a)
    load_w[0].wait()

    def hidden_finish(i, total):
        pre[i] = total
        value = (total * (0.5 * (1.0 + gelu_parts(total)))).astype(BF16)
        p_h[i + 1, pl.ds(1, ny)] = value.reshape(ny, nz, ch)

    conv(z_a, w1, False, hidden_finish)
    halo_start(2, p_h, 1, p_h)
    lhs_h[...] = p_h[pl.ds(1, nx), pl.ds(1, ny)].reshape(cells, ch).T
    halo_wait(1, cot, 0, p_c)
    build(p_c, z_b)
    weight_grad(1, lhs_h, z_b)
    rows_start(1)
    load_w[1].wait()

    def grad_finish(i, total):
        v = pre[i]
        t = gelu_parts(v)
        slope = 0.5 * (1.0 + t) + (0.5 * v) * (1.0 - t * t) * (
            GELU_C * (1.0 + (3.0 * GELU_A) * (v * v))
        )
        p_g[i + 1, pl.ds(1, ny)] = (total * slope).astype(BF16).reshape(ny, nz, ch)

    conv(z_b, w2, True, grad_finish)
    halo_start(3, p_g, 1, p_g)
    halo_wait(2, p_h, 1, p_h)
    build(p_h, z_a)

    def out_finish(i, total):
        out_ref[i] = (
            (fields[i].reshape(tile, ch).astype(F32) + total).astype(BF16).reshape(ny, nz, ch)
        )

    conv(z_a, w2, False, out_finish, 0, nx // 2)
    halo_wait(3, p_g, 1, p_g)
    build(p_g, z_c)
    weight_grad(0, lhs_f, z_c)
    rows_next(1)
    rows_start(0)
    conv(z_a, w2, False, out_finish, nx // 2, nx)
    columns_start(1)

    def field_finish(i, total):
        fgrad_ref[i] = (
            (cot[i].reshape(tile, ch).astype(F32) + total).astype(BF16).reshape(ny, nz, ch)
        )

    conv(z_c, w1, True, field_finish, 0, nx // 2)
    rows_next(0)
    conv(z_c, w1, True, field_finish, nx // 2, nx)
    finish_grad(1, g2_ref)
    columns_start(0)
    finish_grad(0, g1_ref)


def body(sizes, fields, cotangent, first_weight, second_weight):
    ndp, npx, npy = sizes
    batch, nx, ny, nz, ch = fields.shape
    kc = first_weight.shape[0]
    half = ch // npy
    slots = dp_slots(ndp)[1]
    rows = kc // ndp
    rpad = -(-rows // 128) * 128
    wid = ch // (npx * npy)
    cells = nx * ny * nz
    vmem = pl.BlockSpec(memory_space=pltpu.VMEM)
    hbm = pl.BlockSpec(memory_space=pl.ANY)
    padded = pltpu.VMEM((nx + 2, ny + 2, nz, ch), BF16)
    shifted = pltpu.VMEM((nx + 2, ny + 2, nz, 3 * ch), BF16)
    dma = pltpu.SemaphoreType.DMA
    block = (nx, ny, nz, ch)
    out, fgrad, g1, g2 = pl.pallas_call(
        functools.partial(kernel, (ndp, npx, npy, batch * ndp)),
        out_shape=(
            jax.ShapeDtypeStruct(block, BF16),
            jax.ShapeDtypeStruct(block, BF16),
            jax.ShapeDtypeStruct((wid, rpad), F32),
            jax.ShapeDtypeStruct((wid, rpad), F32),
        ),
        in_specs=[vmem, vmem, hbm, hbm],
        out_specs=(vmem, vmem, vmem, vmem),
        scratch_shapes=[
            pltpu.VMEM((kc, ch), BF16),
            pltpu.VMEM((kc, ch), BF16),
            padded, padded, padded, padded,
            shifted, shifted, shifted,
            pltpu.VMEM((ch, cells), BF16),
            pltpu.VMEM((ch, cells), BF16),
            pltpu.VMEM((nx, ny * nz, ch), F32),
            pltpu.VMEM((2, kc, half), F32),
            pltpu.VMEM((2, kc, half), BF16),
            pltpu.VMEM((2, kc, half), BF16),
            pltpu.VMEM((2, len(slots), rows // 2, half), BF16),
            pltpu.VMEM((rpad, half), F32),
            pltpu.VMEM((2, half, rpad), BF16),
            pltpu.VMEM((2, npx, wid, rpad), BF16),
            dma((2,)),
            dma((4, 8)), dma((4, 8)),
            dma((2, 9)), dma((2, 9)),
            dma((2, len(slots))), dma((2, len(slots))),
            dma((2, half // wid)), dma((2, npx)),
        ],
        compiler_params=pltpu.CompilerParams(
            collective_id=0, has_side_effects=True, vmem_limit_bytes=64000000
        ),
        name="closure",
    )(fields.reshape(block), cotangent.reshape(block), first_weight, second_weight)
    out, fgrad, g1, g2 = pl.pallas_call(
        functools.partial(results, rows),
        out_shape=(
            jax.ShapeDtypeStruct(block, BF16),
            jax.ShapeDtypeStruct(block, BF16),
            jax.ShapeDtypeStruct((wid, rows), F32),
            jax.ShapeDtypeStruct((wid, rows), F32),
        ),
        in_specs=[vmem] * 4,
        out_specs=(vmem,) * 4,
        name="results",
    )(out, fgrad, g1, g2)
    return (
        out.reshape(fields.shape),
        fgrad.reshape(fields.shape),
        g1.T,
        g2.T,
    )


def solution(mesh):
    sizes = tuple(mesh.shape[name] for name in ("dp", "px", "py"))
    placed = (P("dp", "px", "py", None, None), P("dp", "px", "py", None, None), P(), P())
    return jax.shard_map(
        functools.partial(body, sizes),
        mesh=mesh,
        in_specs=placed,
        out_specs=(
            P("dp", "px", "py", None, None),
            P("dp", "px", "py", None, None),
            P("dp", ("px", "py")),
            P("dp", ("px", "py")),
        ),
        check_vma=False,
    )
```

```python
import functools

import jax
import jax.numpy as jnp
from jax import lax
from jax.experimental import pallas as pl
from jax.experimental.pallas import tpu as pltpu
from jax.sharding import PartitionSpec as P

MESH = pl.DeviceIdType.MESH
F32, BF16 = jnp.float32, jnp.bfloat16
DIRS = [(dx, dy) for dx in (-1, 0, 1) for dy in (-1, 0, 1) if dx or dy]
GELU_C = 0.7978845608028654
GELU_A = 0.044715


def gelu_parts(v):
    return jnp.tanh(GELU_C * (v + GELU_A * (v * v * v)))


def dp_slots(ndp):
    db = 2 if ndp % 2 == 0 else 1
    da = ndp // db
    first = [(0, 0, hop, item) for hop in range(1, db) for item in [*range(1, da), 0]]
    other = [(0, 1, hop, item) for hop in range(1, da) for item in [*range(1, db), 0]]
    slots = [s for pair in zip(first, other) for s in pair]
    slots += first[len(other) :] + other[len(first) :]
    slots += [(1, 0, hop, 0) for hop in range(1, da)] + [(1, 1, hop, 0) for hop in range(1, db)]
    return (da, db), slots


def results(rows, out_in, fgrad_in, g1_in, g2_in, out_ref, fgrad_ref, g1_ref, g2_ref):
    out_ref[...] = out_in[...]
    fgrad_ref[...] = fgrad_in[...]
    g1_ref[...] = g1_in[:, :rows]
    g2_ref[...] = g2_in[:, :rows]


def kernel(
    sizes,
    fields, cot, w1_hbm, w2_hbm,
    out_ref, fgrad_ref, g1_ref, g2_ref,
    w1, w2, p_f, p_c, p_h, p_g, z_a, z_b, z_c, lhs_f, lhs_h, pre,
    own, send_a, recv_a, recv_b, tot, send_z, recv_z,
    sem_w, halo_send, halo_recv, a_send, a_recv, b_send, b_recv, z_send, z_recv,
):
    ndp, npx, npy, rollouts = sizes
    factors, b_slots = dp_slots(ndp)
    nx, ny, nz, ch = fields.shape
    cells = nx * ny * nz
    half = ch // npy
    rows = own.shape[1] // ndp
    rpad = tot.shape[0]
    wid = recv_z.shape[2]
    nj = half // wid
    d, x, y = lax.axis_index("dp"), lax.axis_index("px"), lax.axis_index("py")

    load_w = [
        pltpu.make_async_copy(w1_hbm, w1, sem_w.at[0]),
        pltpu.make_async_copy(w2_hbm, w2, sem_w.at[1]),
    ]
    for copy in load_w:
        copy.start()

    barrier = pltpu.get_barrier_semaphore()
    for i in range(1, ndp):
        pl.semaphore_signal(
            barrier, inc=1, device_id=(lax.rem(d + i, ndp), x, y), device_id_type=MESH
        )
    for i in range(1, npx * npy):
        other = lax.rem(x * npy + y + i, npx * npy)
        pl.semaphore_signal(
            barrier, inc=1, device_id=(d, other // npy, lax.rem(other, npy)), device_id_type=MESH
        )
    pl.semaphore_wait(barrier, ndp - 1 + npx * npy - 1)

    def exists(dx, dy):
        return (x + dx >= 0) & (x + dx < npx) & (y + dy >= 0) & (y + dy < npy)

    def span_src(step, size, base):
        if step == 0:
            return pl.ds(base, size)
        return pl.ds(base if step < 0 else base + size - 1, 1)

    def span_dst(step, size):
        if step == 0:
            return pl.ds(1, size)
        return pl.ds(size + 1 if step < 0 else 0, 1)

    def halo_copy(which, src, base, padded, index):
        dx, dy = DIRS[index]
        return pltpu.make_async_remote_copy(
            src_ref=src.at[span_src(dx, nx, base), span_src(dy, ny, base)],
            dst_ref=padded.at[span_dst(dx, nx), span_dst(dy, ny)],
            send_sem=halo_send.at[which, index],
            recv_sem=halo_recv.at[which, index],
            device_id=(d, x + dx, y + dy),
            device_id_type=MESH,
        )

    def halo_start(which, src, base, padded):
        for index, (dx, dy) in enumerate(DIRS):
            @pl.when(exists(dx, dy))
            def _():
                halo_copy(which, src, base, padded, index).start()

            @pl.when(jnp.logical_not(exists(-dx, -dy)))
            def _():
                sx, sy = span_dst(dx, nx), span_dst(dy, ny)
                padded[sx, sy] = jnp.zeros((sx.size, sy.size, nz, ch), BF16)

    def halo_wait(which, src, base, padded):
        for index, (dx, dy) in enumerate(DIRS):
            @pl.when(exists(dx, dy))
            def _():
                halo_copy(which, src, base, padded, index).wait_send()

            @pl.when(exists(-dx, -dy))
            def _():
                halo_copy(which, src, base, padded, index).wait_recv()

    def build(padded, shifted):
        @pl.loop(0, nx + 2)
        def _(i):
            plane = padded[i]
            flat = plane.reshape((ny + 2) * nz, ch).astype(F32)
            place = lax.broadcasted_iota(jnp.int32, flat.shape, 0) % nz
            low = jnp.where(place == 0, 0.0, pltpu.roll(flat, 1, 0))
            high = jnp.where(place == nz - 1, 0.0, pltpu.roll(flat, flat.shape[0] - 1, 0))
            shifted[i, :, :, 0:ch] = low.astype(BF16).reshape(plane.shape)
            shifted[i, :, :, ch : 2 * ch] = plane
            shifted[i, :, :, 2 * ch : 3 * ch] = high.astype(BF16).reshape(plane.shape)

    tile = ny * nz

    def conv(shifted, weight, flipped, finish, low=0, high=nx):
        @pl.loop(low, high)
        def _(i):
            total = None
            for a in range(3):
                for b in range(3):
                    first = (9 * a + 3 * b) * ch
                    if not flipped:
                        lhs = shifted[i + a, pl.ds(b, ny)].reshape(tile, 3 * ch)
                        term = jnp.dot(
                            lhs, weight[pl.ds(first, 3 * ch)], preferred_element_type=F32
                        )
                        total = term if total is None else total + term
                        continue
                    for c in range(3):
                        lhs = shifted[
                            i + 2 - a, pl.ds(2 - b, ny), :, pl.ds((2 - c) * ch, ch)
                        ].reshape(tile, ch)
                        term = lax.dot_general(
                            lhs,
                            weight[pl.ds(first + c * ch, ch)],
                            (((1,), (1,)), ((), ())),
                            preferred_element_type=F32,
                        )
                        total = term if total is None else total + term
            finish(i, total)

    partner = 1 - y

    def a_copy(which, step):
        part = pl.ds(pl.multiple_of(step * 3 * ch, 3 * ch), 3 * ch)
        return pltpu.make_async_remote_copy(
            src_ref=send_a.at[which, part],
            dst_ref=recv_a.at[which, part],
            send_sem=a_send.at[which, step],
            recv_sem=a_recv.at[which, step],
            device_id=(d, x, partner),
            device_id_type=MESH,
        )

    def weight_grad(which, lhs, shifted):
        @pl.loop(0, 9)
        def _(step):
            a, b = step // 3, step % 3
            rhs = shifted[pl.ds(2 - a, nx), pl.ds(2 - b, ny)].reshape(cells, 3 * ch)
            prod = jnp.dot(lhs[...], rhs, preferred_element_type=F32)
            for c in range(3):
                block = prod[:, (2 - c) * ch : (3 - c) * ch]
                here = pl.ds(pl.multiple_of(step * 3 * ch, ch) + c * ch, ch)
                low, high = block[:, :half], block[:, half:]
                own[which, here] = jnp.where(y == 0, low, high)
                send_a[which, here] = jnp.where(y == 0, high, low).astype(BF16)
            a_copy(which, step).start()

    da, db = factors
    part_rows = rows // 2
    ia, ib = d // db, lax.rem(d, db)

    def piece(a, b, side):
        first = (a * db + b) * rows + side * part_rows
        return pl.ds(pl.multiple_of(first, 16), part_rows)

    def ring(index, hop, count):
        return lax.rem(index + hop, count)

    def b_copy(which, phase, side, hop, item):
        along_b = (side == 0) == (phase == 0)
        if along_b:
            a, b = (ring(ia, item, da) if phase == 0 else ia), ring(ib, hop, db)
            peer = ia * db + b
        else:
            a, b = ring(ia, hop, da), (ring(ib, item, db) if phase == 0 else ib)
            peer = a * db + ib
        slot = b_slots.index((phase, side, hop, item))
        return piece(a, b, side), pltpu.make_async_remote_copy(
            src_ref=send_a.at[which, piece(a, b, side)],
            dst_ref=recv_b.at[which, slot],
            send_sem=b_send.at[which, slot],
            recv_sem=b_recv.at[which, slot],
            device_id=(peer, x, y),
            device_id_type=MESH,
        )

    def rows_start(which):
        @pl.loop(0, 9)
        def _(step):
            a_copy(which, step).wait()

        for slot in [s for s in b_slots if s[0] == 0]:
            part, copy = b_copy(which, *slot)
            send_a[which, part] = (own[which, part] + recv_a[which, part].astype(F32)).astype(BF16)
            copy.start()
        for side, count in ((0, da), (1, db)):
            for item in range(count):
                a, b = (ring(ia, item, da), ib) if side == 0 else (ia, ring(ib, item, db))
                part = piece(a, b, side)
                own[which, part] = own[which, part] + recv_a[which, part].astype(F32)

    def rows_next(which):
        for side, count, hops in ((0, da, db), (1, db, da)):
            for item in [*range(1, count), 0]:
                a, b = (ring(ia, item, da), ib) if side == 0 else (ia, ring(ib, item, db))
                part = piece(a, b, side)
                total = own[which, part]
                for hop in range(1, hops):
                    slot = (0, side, hop, item)
                    b_copy(which, *slot)[1].wait()
                    total = total + recv_b[which, b_slots.index(slot)].astype(F32)
                if item:
                    send_a[which, part] = total.astype(BF16)
                    b_copy(which, 1, side, item, 0)[1].start()
                else:
                    own[which, part] = total

    def z_ids(j):
        owner = y * nj + j
        return owner // npy, lax.rem(owner, npy)

    def z_remote(which, j):
        px_o, py_o = z_ids(j)
        return pltpu.make_async_remote_copy(
            src_ref=send_z.at[which, pl.ds(j * wid, wid)],
            dst_ref=recv_z.at[which, x],
            send_sem=z_send.at[which, j],
            recv_sem=z_recv.at[which, x],
            device_id=(d, px_o, py_o),
            device_id_type=MESH,
        )

    def columns_start(which):
        for side, hops in ((0, da), (1, db)):
            total = own[which, piece(ia, ib, side)]
            for hop in range(1, hops):
                slot = (1, side, hop, 0)
                b_copy(which, *slot)[1].wait()
                total = total + recv_b[which, b_slots.index(slot)].astype(F32)
            tot[side * part_rows : (side + 1) * part_rows] = total
        if rpad > rows:
            tot[rows:rpad] = jnp.zeros((rpad - rows, half), F32)
        send_z[which] = tot[...].T.astype(BF16)
        for j in range(nj):
            px_o, py_o = z_ids(j)
            mine = (px_o == x) & (py_o == y)

            @pl.when(jnp.logical_not(mine))
            def _():
                z_remote(which, j).start()

            @pl.when(mine)
            def _():
                pltpu.make_async_copy(
                    send_z.at[which, pl.ds(j * wid, wid)], recv_z.at[which, x], z_recv.at[which, x]
                ).start()

    def finish_grad(which, grad):
        for j in range(nj):
            px_o, py_o = z_ids(j)

            @pl.when(jnp.logical_not((px_o == x) & (py_o == y)))
            def _():
                z_remote(which, j).wait_send()

        total = None
        for i in range(npx):
            pltpu.make_async_copy(
                recv_z.at[which, i], recv_z.at[which, i], z_recv.at[which, i]
            ).wait()
            term = recv_z[which, i].astype(F32)
            total = term if total is None else total + term
        grad[...] = total / rollouts

    halo_start(0, fields, 0, p_f)
    halo_start(1, cot, 0, p_c)
    p_f[pl.ds(1, nx), pl.ds(1, ny)] = fields[...]
    p_c[pl.ds(1, nx), pl.ds(1, ny)] = cot[...]
    lhs_f[...] = fields[...].reshape(cells, ch).T
    halo_wait(0, fields, 0, p_f)
    build(p_f, z_a)
    load_w[0].wait()

    def hidden_finish(i, total):
        pre[i] = total
        value = (total * (0.5 * (1.0 + gelu_parts(total)))).astype(BF16)
        p_h[i + 1, pl.ds(1, ny)] = value.reshape(ny, nz, ch)

    conv(z_a, w1, False, hidden_finish)
    halo_start(2, p_h, 1, p_h)
    lhs_h[...] = p_h[pl.ds(1, nx), pl.ds(1, ny)].reshape(cells, ch).T
    halo_wait(1, cot, 0, p_c)
    build(p_c, z_b)
    weight_grad(1, lhs_h, z_b)
    rows_start(1)
    load_w[1].wait()

    def grad_finish(i, total):
        v = pre[i]
        t = gelu_parts(v)
        slope = 0.5 * (1.0 + t) + (0.5 * v) * (1.0 - t * t) * (
            GELU_C * (1.0 + (3.0 * GELU_A) * (v * v))
        )
        p_g[i + 1, pl.ds(1, ny)] = (total * slope).astype(BF16).reshape(ny, nz, ch)

    conv(z_b, w2, True, grad_finish)
    halo_start(3, p_g, 1, p_g)
    halo_wait(2, p_h, 1, p_h)
    build(p_h, z_a)

    def out_finish(i, total):
        out_ref[i] = (
            (fields[i].reshape(tile, ch).astype(F32) + total).astype(BF16).reshape(ny, nz, ch)
        )

    conv(z_a, w2, False, out_finish, 0, nx // 2)
    halo_wait(3, p_g, 1, p_g)
    build(p_g, z_c)
    rows_next(1)
    weight_grad(0, lhs_f, z_c)
    rows_start(0)
    columns_start(1)
    conv(z_a, w2, False, out_finish, nx // 2, nx)

    def field_finish(i, total):
        fgrad_ref[i] = (
            (cot[i].reshape(tile, ch).astype(F32) + total).astype(BF16).reshape(ny, nz, ch)
        )

    conv(z_c, w1, True, field_finish, 0, nx // 2)
    rows_next(0)
    conv(z_c, w1, True, field_finish, nx // 2, nx)
    finish_grad(1, g2_ref)
    columns_start(0)
    finish_grad(0, g1_ref)


def body(sizes, fields, cotangent, first_weight, second_weight):
    ndp, npx, npy = sizes
    batch, nx, ny, nz, ch = fields.shape
    kc = first_weight.shape[0]
    half = ch // npy
    slots = dp_slots(ndp)[1]
    rows = kc // ndp
    rpad = -(-rows // 128) * 128
    wid = ch // (npx * npy)
    cells = nx * ny * nz
    vmem = pl.BlockSpec(memory_space=pltpu.VMEM)
    hbm = pl.BlockSpec(memory_space=pl.ANY)
    padded = pltpu.VMEM((nx + 2, ny + 2, nz, ch), BF16)
    shifted = pltpu.VMEM((nx + 2, ny + 2, nz, 3 * ch), BF16)
    dma = pltpu.SemaphoreType.DMA
    block = (nx, ny, nz, ch)
    out, fgrad, g1, g2 = pl.pallas_call(
        functools.partial(kernel, (ndp, npx, npy, batch * ndp)),
        out_shape=(
            jax.ShapeDtypeStruct(block, BF16),
            jax.ShapeDtypeStruct(block, BF16),
            jax.ShapeDtypeStruct((wid, rpad), F32),
            jax.ShapeDtypeStruct((wid, rpad), F32),
        ),
        in_specs=[vmem, vmem, hbm, hbm],
        out_specs=(vmem, vmem, vmem, vmem),
        scratch_shapes=[
            pltpu.VMEM((kc, ch), BF16),
            pltpu.VMEM((kc, ch), BF16),
            padded, padded, padded, padded,
            shifted, shifted, shifted,
            pltpu.VMEM((ch, cells), BF16),
            pltpu.VMEM((ch, cells), BF16),
            pltpu.VMEM((nx, ny * nz, ch), F32),
            pltpu.VMEM((2, kc, half), F32),
            pltpu.VMEM((2, kc, half), BF16),
            pltpu.VMEM((2, kc, half), BF16),
            pltpu.VMEM((2, len(slots), rows // 2, half), BF16),
            pltpu.VMEM((rpad, half), F32),
            pltpu.VMEM((2, half, rpad), BF16),
            pltpu.VMEM((2, npx, wid, rpad), BF16),
            dma((2,)),
            dma((4, 8)), dma((4, 8)),
            dma((2, 9)), dma((2, 9)),
            dma((2, len(slots))), dma((2, len(slots))),
            dma((2, half // wid)), dma((2, npx)),
        ],
        compiler_params=pltpu.CompilerParams(
            collective_id=0, has_side_effects=True, vmem_limit_bytes=64000000
        ),
        name="closure",
    )(fields.reshape(block), cotangent.reshape(block), first_weight, second_weight)
    out, fgrad, g1, g2 = pl.pallas_call(
        functools.partial(results, rows),
        out_shape=(
            jax.ShapeDtypeStruct(block, BF16),
            jax.ShapeDtypeStruct(block, BF16),
            jax.ShapeDtypeStruct((wid, rows), F32),
            jax.ShapeDtypeStruct((wid, rows), F32),
        ),
        in_specs=[vmem] * 4,
        out_specs=(vmem,) * 4,
        name="results",
    )(out, fgrad, g1, g2)
    return (
        out.reshape(fields.shape),
        fgrad.reshape(fields.shape),
        g1.T,
        g2.T,
    )


def solution(mesh):
    sizes = tuple(mesh.shape[name] for name in ("dp", "px", "py"))
    placed = (P("dp", "px", "py", None, None), P("dp", "px", "py", None, None), P(), P())
    return jax.shard_map(
        functools.partial(body, sizes),
        mesh=mesh,
        in_specs=placed,
        out_specs=(
            P("dp", "px", "py", None, None),
            P("dp", "px", "py", None, None),
            P("dp", ("px", "py")),
            P("dp", ("px", "py")),
        ),
        check_vma=False,
    )
```
